32 devices in a mesh: fsdp: 32 (over z, y, x, core).
Axes of the slice: x: 2, y: 2, z: 4, core: 2. Of those that a mesh axis runs over, the one named last changes fastest.
Arguments:
- query_states: bfloat16 [64, 64, 768], P('fsdp'), may hold values from -6 to 6
- passage_states: bfloat16 [64, 512, 768], P('fsdp'), may hold values from -6 to 6
- query_lengths: int32 [64], P('fsdp'), may hold values from 8 to 64, as said below
- passage_lengths: int32 [64], P('fsdp'), may hold values from 64 to 512, as said below
- positive_index: int32 [64], P('fsdp'), may hold values from 0 to 63, each once
- query_weight: bfloat16 [768, 768], P('fsdp'), may hold values from -0.21875 to 0.21875
- query_bias: bfloat16 [768], P('fsdp'), may hold values from -1 to 1
- key_weight: bfloat16 [768, 768], P('fsdp'), may hold values from -0.21875 to 0.21875
- value_weight: bfloat16 [768, 768], P('fsdp'), may hold values from -0.21875 to 0.21875
- value_bias: bfloat16 [768], P('fsdp'), may hold values from -1 to 1
- out_weight: bfloat16 [768, 768], P('fsdp'), may hold values from -1.75 to 1.75
- out_bias: bfloat16 [768], P('fsdp'), may hold values from -1 to 1
- first_gain: bfloat16 [768], P('fsdp'), may hold values from 0.5 to 1.5
- first_shift: bfloat16 [768], P('fsdp'), may hold values from -0.29882812 to 0.29882812
- inner_weight: bfloat16 [768, 3072], P('fsdp'), may hold values from -0.21875 to 0.21875
- inner_bias: bfloat16 [3072], P('fsdp'), may hold values from -1 to 1
- down_weight: bfloat16 [3072, 768], P('fsdp'), may hold values from -0.109375 to 0.109375
- down_bias: bfloat16 [768], P('fsdp'), may hold values from -1 to 1
- second_gain: bfloat16 [768], P('fsdp'), may hold values from 0.5 to 1.5
- second_shift: bfloat16 [768], P('fsdp'), may hold values from -0.29882812 to 0.29882812
Outputs:
- loss_value: float32 [], replicated
- question_embedding_array: float32 [64, 768], P('fsdp')
- document_embedding_array: float32 [64, 768], P('fsdp')
- query_grad: bfloat16 [64, 64, 768], P('fsdp')
- passage_grad: bfloat16 [64, 512, 768], P('fsdp')
- query_weight_grad: float32 [768, 768], P('fsdp')
- query_bias_grad: float32 [768], P('fsdp')
- key_weight_grad: float32 [768, 768], P('fsdp')
- value_weight_grad: float32 [768, 768], P('fsdp')
- value_bias_grad: float32 [768], P('fsdp')
- out_weight_grad: float32 [768, 768], P('fsdp')
- out_bias_grad: float32 [768], P('fsdp')
- first_gain_grad: float32 [768], P('fsdp')
- first_shift_grad: float32 [768], P('fsdp')
- inner_weight_grad: float32 [768, 3072], P('fsdp')
- inner_bias_grad: float32 [3072], P('fsdp')
- down_weight_grad: float32 [3072, 768], P('fsdp')
- down_bias_grad: float32 [768], P('fsdp')
- second_gain_grad: float32 [768], P('fsdp')
- second_shift_grad: float32 [768], P('fsdp')
The draws below stay inside these ranges and needn't reach their ends.
Inputs may be any that keep to these rules, and one draw needn't show every extreme that they name: `query_lengths`: true length of each query; some query has exactly 64. `passage_lengths`: true length of each passage; some passage has exactly 512. `positive_index`: each passage is the positive of exactly one query.
All inputs are finite; a program needn't handle non-finite values.
Results may differ from the reference program's by a relative error of at most 0.013.
Values may be sent and summed in bfloat16 or wider, within the bound.
No kernel may reach another device: no remote copies, remote signals or barrier semaphores. Data moves between devices by JAX's collectives and lax.ppermute only.
A program may use at most 192 MiB of HBM per device.

```python
import jax
import jax.numpy as jnp
from jax import lax

D = 768
HEADS = 12
HEAD_DIM = 64
FF = 3072
QLEN = 64
PLEN = 512
PAIRS = 64


def draw_query_lengths(key, part):
    drawn = jax.random.randint(key, (PAIRS,), QLEN // 8, QLEN + 1, dtype=jnp.int32)
    place = jax.random.randint(jax.random.fold_in(key, 7), (), 0, PAIRS, dtype=jnp.int32)
    return drawn.at[place].set(QLEN)


def draw_passage_lengths(key, part):
    drawn = jax.random.randint(key, (PAIRS,), PLEN // 8, PLEN + 1, dtype=jnp.int32)
    place = jax.random.randint(jax.random.fold_in(key, 11), (), 0, PAIRS, dtype=jnp.int32)
    return drawn.at[place].set(PLEN)


def levels(key, shape, cuts, least, largest):
    level, own = 1.0, jax.random.fold_in(key, 6)
    for position, blocks in cuts:
        heights = jnp.exp(jax.random.uniform(jax.random.fold_in(own, position), (blocks,), jnp.float32, least / len(cuts), largest / len(cuts)))
        level = level * jnp.repeat(heights, shape[position] // blocks).reshape([-1 if axis == position else 1 for axis in range(len(shape))])
    return level


def gaussian(own_key, shape, width, most, split=(), kind=jnp.bfloat16):
    level = levels(own_key, shape, split, -0.22, 0.18) if split else 1.0
    values = jax.random.normal(own_key, shape, jnp.float32) * width * level
    return jnp.minimum(jnp.maximum(values, -most), most).astype(kind)


def setup_inputs(seed: int = 0) -> dict:
    keys = jax.random.split(jax.random.key(seed), 21)
    return {
        "query_states": gaussian(keys[0], (PAIRS, QLEN, D), 1.0, 6.0, ((0, 32),)),
        "passage_states": gaussian(keys[1], (PAIRS, PLEN, D), 1.0, 6.0, ((0, 32),)),
        "query_lengths": draw_query_lengths(jax.random.fold_in(keys[20], 71), 0),
        "passage_lengths": draw_passage_lengths(jax.random.fold_in(keys[20], 71), 0),
        "positive_index": jax.random.permutation(keys[4], PAIRS).astype(jnp.int32),
        "query_weight": gaussian(keys[5], (D, D), D ** -0.5, 0.21875, ((0, 32),)),
        "query_bias": gaussian(keys[6], (D,), 0.2, 1.0, ((0, 32),)),
        "key_weight": gaussian(keys[7], (D, D), D ** -0.5, 0.21875, ((0, 32),)),
        "value_weight": gaussian(keys[8], (D, D), D ** -0.5, 0.21875, ((0, 32),)),
        "value_bias": gaussian(keys[9], (D,), 0.2, 1.0, ((0, 32),)),
        "out_weight": gaussian(keys[10], (D, D), (D // 64) ** -0.5, 1.75, ((0, 32),)),
        "out_bias": gaussian(keys[11], (D,), 0.2, 1.0, ((0, 32),)),
        "first_gain": jnp.clip(1.0 + 0.1 * jax.random.normal(keys[12], (D,), jnp.float32), 0.5, 1.5).astype(jnp.bfloat16),
        "first_shift": gaussian(keys[13], (D,), 0.05, 0.29882812, ((0, 32),)),
        "inner_weight": gaussian(keys[14], (D, FF), D ** -0.5, 0.21875, ((0, 32),)),
        "inner_bias": gaussian(keys[15], (FF,), 0.2, 1.0, ((0, 32),)),
        "down_weight": gaussian(keys[16], (FF, D), FF ** -0.5, 0.109375, ((0, 32),)),
        "down_bias": gaussian(keys[17], (D,), 0.2, 1.0, ((0, 32),)),
        "second_gain": jnp.clip(1.0 + 0.1 * jax.random.normal(keys[18], (D,), jnp.float32), 0.5, 1.5).astype(jnp.bfloat16),
        "second_shift": gaussian(keys[19], (D,), 0.05, 0.29882812, ((0, 32),)),
    }


sharpness_divisor = 0.01
epsilon = 1e-12

@jax.custom_vjp
def low(v):
    return lax.optimization_barrier(v.astype(jnp.bfloat16)).astype(jnp.float32)

@jax.custom_vjp
def low_back(v):
    return v

def low_keep(v):
    return (low(v), None)

def low_pass(kept, grad):
    return (grad,)

def back_keep(v):
    return (v, None)

def back_low(kept, grad):
    return (low(grad),)
low.defvjp(low_keep, low_pass)
low_back.defvjp(back_keep, back_low)

def round_both(value):
    return low_back(low(value))

def bilinear_outcome(formula, left_side, right_side):
    return jnp.einsum(formula, left_side, right_side, precision=lax.Precision.HIGHEST)

def normalize(hidden, gain_vec, shift_vec):
    row_mean = lax.optimization_barrier(jnp.mean(hidden, axis=-1, keepdims=True))
    centered = hidden - row_mean
    variance = lax.optimization_barrier(jnp.mean(centered * centered, axis=-1, keepdims=True))
    return centered * lax.rsqrt(variance + epsilon) * gain_vec + shift_vec

def gelu_exact(inputs):
    return jax.nn.gelu(inputs, approximate=False)

def encode(states, length, weight_set):
    query_weight, query_bias, key_weight, value_weight, value_bias, out_weight, out_bias, first_gain, first_shift, inner_weight, inner_bias, down_weight, down_bias, second_gain, second_shift = weight_set
    seq_len = states.shape[0]
    key_valid = jnp.arange(seq_len, dtype=jnp.int32) < length
    queries = round_both(bilinear_outcome('td,de->te', states, query_weight) + query_bias).reshape(seq_len, HEADS, HEAD_DIM)
    keys_low = round_both(bilinear_outcome('td,de->te', states, key_weight)).reshape(seq_len, HEADS, HEAD_DIM)
    values_low = round_both(bilinear_outcome('td,de->te', states, value_weight) + value_bias).reshape(seq_len, HEADS, HEAD_DIM)
    scores = low_back(bilinear_outcome('qhd,khd->hqk', queries, keys_low) * 0.125)
    scores = jnp.where(key_valid[None, None, :], scores, -1000000000.0)
    probs_low = low(jax.nn.softmax(scores, axis=-1))
    mixed_heads = round_both(bilinear_outcome('hqk,khd->qhd', probs_low, values_low).reshape(seq_len, D))
    attended = low_back(bilinear_outcome('td,de->te', mixed_heads, out_weight) + out_bias)
    leading_norm = normalize(states + attended, first_gain, first_shift)
    inner_sum = low_back(bilinear_outcome('td,de->te', low(leading_norm), inner_weight) + inner_bias)
    activated = low(gelu_exact(inner_sum))
    outer_sum = low_back(bilinear_outcome('td,de->te', activated, down_weight) + down_bias)
    final_norm = normalize(leading_norm + outer_sum, second_gain, second_shift)
    pooled = lax.optimization_barrier(jnp.sum(jnp.where(key_valid[:, None], final_norm, 0.0), axis=0))
    return pooled / length.astype(jnp.float32)

def encode_pair(weight_set, pieces):
    query_rows, passage_rows, query_length, passage_length = pieces
    return (encode(query_rows, query_length, weight_set), encode(passage_rows, passage_length, weight_set))

def unit_length_entries(embed):
    return embed * lax.rsqrt(lax.optimization_barrier(jnp.sum(embed * embed, axis=-1, keepdims=True)) + 1e-06)

def contrast(question_embedding_array, document_embedding_array, positive_index):
    similarity_scores_grid = bilinear_outcome('fo,no->fn', unit_length_entries(question_embedding_array), unit_length_entries(document_embedding_array)) / sharpness_divisor
    picked = jnp.take_along_axis(similarity_scores_grid, positive_index[:, None], axis=1)[:, 0]
    return jnp.mean(jax.nn.logsumexp(similarity_scores_grid, axis=1) - picked)

def reference(query_states, passage_states, query_lengths, passage_lengths, positive_index, query_weight, query_bias, key_weight, value_weight, value_bias, out_weight, out_bias, first_gain, first_shift, inner_weight, inner_bias, down_weight, down_bias, second_gain, second_shift):
    weight_set = tuple((weight_arg.astype(jnp.float32) for weight_arg in (query_weight, query_bias, key_weight, value_weight, value_bias, out_weight, out_bias, first_gain, first_shift, inner_weight, inner_bias, down_weight, down_bias, second_gain, second_shift)))
    query_float = query_states.astype(jnp.float32)
    passage_float = passage_states.astype(jnp.float32)

    def objective(weight_tuple, query_input, passage_input):

        def pair_step(pieces):
            return encode_pair(weight_tuple, pieces)
        question_embedding_array, document_embedding_array = lax.map(jax.checkpoint(pair_step), (query_input, passage_input, query_lengths, passage_lengths))
        return (contrast(question_embedding_array, document_embedding_array, positive_index), (question_embedding_array, document_embedding_array))
    loss_value, pullback, embeds = jax.vjp(objective, weight_set, query_float, passage_float, has_aux=True)
    weight_grads, query_grad, passage_grad = pullback(jnp.ones_like(loss_value))
    return (loss_value, embeds[0], embeds[1], query_grad.astype(jnp.bfloat16), passage_grad.astype(jnp.bfloat16), weight_grads[0], weight_grads[1], weight_grads[2], weight_grads[3], weight_grads[4], weight_grads[5], weight_grads[6], weight_grads[7], weight_grads[8], weight_grads[9], weight_grads[10], weight_grads[11], weight_grads[12], weight_grads[13], weight_grads[14])
```

```python
import functools

import jax
import jax.numpy as jnp
from jax import lax
from jax.experimental import pallas as pl
from jax.experimental.pallas import tpu as pltpu
from jax.sharding import PartitionSpec as P

HEAD_DIM = 64
AXIS = "fsdp"
epsilon = 1e-12
sharpness_divisor = 0.01
masked_score = -1000000000.0
bf16 = jnp.bfloat16
f32 = jnp.float32


class Grid:
    def __init__(self, total):
        self.total = total
        chips = total // 2
        self.outer = 4 if chips % 4 == 0 else 1
        self.inner = chips // self.outer
        me = lax.axis_index(AXIS)
        self.o = me // (2 * self.inner)
        self.i = (me // 2) % self.inner
        self.c = me % 2

    def swap(self, value, mask):
        return lax.ppermute(value, AXIS, [(d, d ^ mask) for d in range(self.total)])

    def masks(self, which):
        if which == "o":
            return [(m, m * 2 * self.inner) for m in range(1, self.outer)]
        return [(m, m * 2) for m in range(1, self.inner)]


def put(buffer, value, index, axis):
    return lax.dynamic_update_slice_in_dim(buffer, value, index, axis)


def gather_chips(grid, block, order):
    shape = block.shape
    if order == "oi":
        first = jnp.zeros((grid.outer, 1) + shape, block.dtype)
        first = put(first, block[None, None], grid.o, 0)
        for m, mask in grid.masks("o"):
            first = put(first, grid.swap(block, mask)[None, None], grid.o ^ m, 0)
        second = jnp.zeros((grid.outer, grid.inner) + shape, block.dtype)
        second = put(second, first, grid.i, 1)
        for m, mask in grid.masks("i"):
            second = put(second, grid.swap(first, mask), grid.i ^ m, 1)
    else:
        first = jnp.zeros((1, grid.inner) + shape, block.dtype)
        first = put(first, block[None, None], grid.i, 1)
        for m, mask in grid.masks("i"):
            first = put(first, grid.swap(block, mask)[None, None], grid.i ^ m, 1)
        second = jnp.zeros((grid.outer, grid.inner) + shape, block.dtype)
        second = put(second, first, grid.o, 0)
        for m, mask in grid.masks("o"):
            second = put(second, grid.swap(first, mask), grid.o ^ m, 0)
    return second


def gather_all(grid, block, order):
    mine = gather_chips(grid, block, order)
    other = grid.swap(mine, 1)
    return mine, other


def interleave(grid, pair, start, count):
    mine, other = (part[:, :, start : start + count] for part in pair)
    even = jnp.where(grid.c == 0, mine, other)
    odd = jnp.where(grid.c == 0, other, mine)
    both = jnp.stack([even, odd], axis=2)
    return both.reshape(grid.total, count, mine.shape[-1])


def scatter_sum(grid, parts, order):
    send = lax.dynamic_index_in_dim(parts, 1 - grid.c, 2, keepdims=False)
    keep = lax.dynamic_index_in_dim(parts, grid.c, 2, keepdims=False)
    kept = (keep.astype(f32) + grid.swap(send, 1).astype(f32)).astype(bf16)
    axes = (1, 0) if order == "io" else (0, 1)
    for axis in axes:
        which, mine = (("o", grid.o), ("i", grid.i))[axis]
        total = lax.dynamic_index_in_dim(kept, mine, axis, keepdims=True).astype(f32)
        for m, mask in grid.masks(which):
            piece = lax.dynamic_index_in_dim(kept, mine ^ m, axis, keepdims=True)
            total = total + grid.swap(piece, mask).astype(f32)
        kept = total if axis == axes[-1] else total.astype(bf16)
    return kept.reshape(kept.shape[2:])


def dot(a, b, ca, cb):
    return lax.dot_general(a, b, (((ca,), (cb,)), ((), ())), preferred_element_type=f32)


def lane_half(value, half):
    lane = lax.broadcasted_iota(jnp.int32, value.shape, 1)
    keep = lane < HEAD_DIM if half == 0 else lane >= HEAD_DIM
    return jnp.where(keep, value, jnp.zeros_like(value))


def sequences(passages, passage_rows, queries, query_rows):
    spans = [(j * passage_rows, passage_rows, (j,)) for j in range(passages)]
    return spans, (passages * passage_rows, queries * query_rows)


def key_masks(span, plen_ref, qlen_ref, sizes):
    start, rows, index = span
    passages, passage_rows, queries, query_rows = sizes
    if index is not None:
        key = lax.broadcasted_iota(jnp.int32, (rows, 1), 0)
        return key < plen_ref[index]
    key = lax.broadcasted_iota(jnp.int32, (rows, rows), 0)
    query = lax.broadcasted_iota(jnp.int32, (rows, rows), 1)
    valid = jnp.zeros((rows, rows), jnp.bool_)
    for j in range(queries):
        low, high = j * query_rows, (j + 1) * query_rows
        valid = valid | (
            (key >= low) & (key < low + qlen_ref[j]) & (query >= low) & (query < high)
        )
    return valid


def spans_of(sizes):
    passages, passage_rows, queries, query_rows = sizes
    spans = [(j * passage_rows, passage_rows, j) for j in range(passages)]
    spans.append((passages * passage_rows, queries * query_rows, None))
    return spans


def attention_forward_kernel(sizes, plen_ref, qlen_ref, q_ref, k_ref, v_ref, mixed_ref, lse_ref):
    for span in spans_of(sizes):
        start, rows, _ = span
        here = pl.ds(start, rows)
        q = q_ref[here, :] * jnp.asarray(0.125, bf16)
        k = k_ref[here, :]
        v = v_ref[here, :]
        valid = key_masks(span, plen_ref, qlen_ref, sizes)
        outs = []
        for half in range(2):
            scores = dot(lane_half(k, half), q, 1, 1)
            scores = jnp.where(valid, scores, masked_score)
            top = jnp.max(scores, axis=0, keepdims=True)
            weights = jnp.exp(scores - top)
            total = jnp.sum(weights, axis=0, keepdims=True)
            probs_low = (weights * (1.0 / total)).astype(bf16)
            lse_ref[0, pl.ds(half, 1), here] = top + jnp.log(total)
            outs.append(dot(v, probs_low, 0, 0)[half * HEAD_DIM : (half + 1) * HEAD_DIM])
        mixed_ref[here, :] = jnp.concatenate(outs, axis=0).T.astype(bf16)


def attention_backward_kernel(
    sizes, plen_ref, qlen_ref, q_ref, k_ref, v_ref, g_ref, lse_ref, dq_ref, dk_ref, dv_ref
):
    for span in spans_of(sizes):
        start, rows, _ = span
        here = pl.ds(start, rows)
        q = q_ref[here, :]
        scaled = q * jnp.asarray(0.125, bf16)
        k = k_ref[here, :]
        v = v_ref[here, :]
        g = g_ref[here, :]
        valid = key_masks(span, plen_ref, qlen_ref, sizes)
        lane = lax.broadcasted_iota(jnp.int32, (rows, 2 * HEAD_DIM), 1)
        dqs, dks, dvs = [], [], []
        for half in range(2):
            scores = dot(lane_half(k, half), scaled, 1, 1)
            lse = lse_ref[0, pl.ds(half, 1), here]
            probs = jnp.where(valid, jnp.exp(jnp.minimum(scores - lse, 0.5)), 0.0)
            prob_grad = dot(lane_half(v, half), g, 1, 1)
            row_dot = jnp.sum(prob_grad * probs, axis=0, keepdims=True)
            score_low = (probs * (prob_grad - row_dot)).astype(bf16)
            dvs.append(dot(probs.astype(bf16), g, 1, 0))
            dks.append(dot(score_low, scaled, 1, 0))
            dqs.append(dot(k, score_low, 0, 0)[half * HEAD_DIM : (half + 1) * HEAD_DIM])
        low = lane < HEAD_DIM
        dv_ref[here, :] = jnp.where(low, dvs[0], dvs[1]).astype(bf16)
        dk_ref[here, :] = jnp.where(low, dks[0], dks[1]).astype(bf16)
        dq_ref[here, :] = (jnp.concatenate(dqs, axis=0).T * 0.125).astype(bf16)


def attention_call(kernel, sizes, arrays, lse, outs, name):
    tokens, width = arrays[0].shape
    pairs = width // (2 * HEAD_DIM)
    block = pl.BlockSpec((tokens, 2 * HEAD_DIM), lambda h, *_: (0, h))
    lse_block = pl.BlockSpec((1, 2, tokens), lambda h, *_: (h, 0, 0))
    wide = jax.ShapeDtypeStruct((tokens, width), bf16)
    lse_shape = jax.ShapeDtypeStruct((pairs, 2, tokens), f32)
    return pl.pallas_call(
        functools.partial(kernel, sizes),
        grid_spec=pltpu.PrefetchScalarGridSpec(
            num_scalar_prefetch=2,
            grid=(pairs,),
            in_specs=[block] * (len(arrays) - 2) + ([lse_block] if lse is not None else []),
            out_specs=[block if o == "wide" else lse_block for o in outs],
        ),
        out_shape=[wide if o == "wide" else lse_shape for o in outs],
        compiler_params=pltpu.CompilerParams(vmem_limit_bytes=56 << 20),
        name=name,
    )


def attention_forward(sizes, plen, qlen, q, k, v):
    call = attention_call(
        attention_forward_kernel, sizes, (q, k, v, None, None), None, ("wide", "lse"), "attn_fwd"
    )
    return call(plen, qlen, q, k, v)


def attention_backward(sizes, plen, qlen, q, k, v, g, lse):
    call = attention_call(
        attention_backward_kernel,
        sizes,
        (q, k, v, g, None, None),
        lse,
        ("wide", "wide", "wide"),
        "attn_bwd",
    )
    return call(plen, qlen, q, k, v, g, lse)


def project(left_side, right_side):
    return dot(left_side, right_side, 1, 0)


def project_back(left_side, right_side):
    return dot(left_side, right_side, 1, 1)


def weight_grad(left_side, right_side):
    return dot(left_side, right_side, 0, 0)


def column_sum(rounded):
    return jnp.sum(rounded.astype(f32), axis=0)


def standardize(hidden):
    row_mean = jnp.mean(hidden, axis=-1, keepdims=True)
    centered = hidden - row_mean
    variance = jnp.mean(centered * centered, axis=-1, keepdims=True)
    inverse = lax.rsqrt(variance + epsilon)
    return centered * inverse, inverse


def standardize_back(grad, unit, inverse):
    return inverse * (
        grad
        - jnp.mean(grad, axis=-1, keepdims=True)
        - unit * jnp.mean(grad * unit, axis=-1, keepdims=True)
    )


def gelu_and_slope(inputs):
    cdf = 0.5 * (1.0 + lax.erf(inputs * 0.7071067811865476))
    density = jnp.exp(-0.5 * inputs * inputs) * 0.3989422804014327
    return inputs * cdf, cdf + inputs * density


def unit_rows(embed):
    scale = lax.rsqrt(jnp.sum(embed * embed, axis=-1, keepdims=True) + 1e-06)
    return embed * scale, scale


def unit_rows_back(grad, unit, scale):
    return scale * (grad - unit * jnp.sum(grad * unit, axis=-1, keepdims=True))


def exact(left_side, right_side, ca, cb):
    return lax.dot_general(
        left_side,
        right_side,
        (((ca,), (cb,)), ((), ())),
        precision=lax.Precision.HIGHEST,
        preferred_element_type=f32,
    )


def on_device(
    total,
    query_states,
    passage_states,
    query_lengths,
    passage_lengths,
    positive_index,
    query_weight,
    query_bias,
    key_weight,
    value_weight,
    value_bias,
    out_weight,
    out_bias,
    first_gain,
    first_shift,
    inner_weight,
    inner_bias,
    down_weight,
    down_bias,
    second_gain,
    second_shift,
):
    grid = Grid(total)
    width = query_weight.shape[1]
    rows = query_weight.shape[0]
    hidden = inner_weight.shape[1]
    folds = hidden // width
    queries, query_rows, _ = query_states.shape
    passages, passage_rows, _ = passage_states.shape
    sizes = (passages, passage_rows, queries, query_rows)
    pad_rows = -(-(9 * rows + folds * rows) // width)
    pad_rows = -(-pad_rows // 8) * 8

    small = jnp.concatenate(
        [
            query_bias,
            value_bias,
            out_bias,
            first_gain,
            first_shift,
            down_bias,
            second_gain,
            second_shift,
            inner_bias,
        ]
    )
    small = jnp.pad(small, (0, pad_rows * width - small.size)).reshape(pad_rows, width)
    inner_folds = jnp.concatenate(
        [inner_weight[:, j * width : (j + 1) * width] for j in range(folds)], axis=0
    )
    attention_one = jnp.concatenate([query_weight, key_weight, value_weight, small], axis=0)
    cut = (folds + 1) * rows
    forward_block = jnp.concatenate([inner_folds, down_weight], axis=0)

    pair_one = gather_all(grid, attention_one, "oi")
    pair_two = gather_all(grid, out_weight, "io")
    pair_three = gather_all(grid, forward_block[:cut], "oi")
    pair_four = gather_all(grid, forward_block[cut:], "io")

    whole_query = interleave(grid, pair_one, 0, rows).reshape(width, width)
    whole_key = interleave(grid, pair_one, rows, rows).reshape(width, width)
    whole_value = interleave(grid, pair_one, 2 * rows, rows).reshape(width, width)
    whole_small = interleave(grid, pair_one, 3 * rows, pad_rows).reshape(total, pad_rows * width)
    whole_out = interleave(grid, pair_two, 0, rows).reshape(width, width)
    whole_inner = jnp.concatenate(
        [interleave(grid, pair_three, j * rows, rows).reshape(width, width) for j in range(folds)],
        axis=1,
    )
    down_parts = [interleave(grid, pair_three, folds * rows, rows)]
    down_parts.append(interleave(grid, pair_four, 0, (folds - 1) * rows))
    whole_down = jnp.concatenate(down_parts, axis=1).reshape(hidden, width)

    def vector(j, count=1):
        return whole_small[:, j * rows : (j + count) * rows].reshape(-1).astype(f32)

    (w_query_bias, w_value_bias, w_out_bias, w_first_gain, w_first_shift) = (
        vector(j) for j in range(5)
    )
    (w_down_bias, w_second_gain, w_second_shift) = (vector(j) for j in range(5, 8))
    w_inner_bias = vector(8, folds)

    states = jnp.concatenate(
        [passage_states.reshape(-1, width), query_states.reshape(-1, width)], axis=0
    )
    q = (project(states, whole_query) + w_query_bias).astype(bf16)
    k = project(states, whole_key).astype(bf16)
    v = (project(states, whole_value) + w_value_bias).astype(bf16)
    mixed, lse = attention_forward(sizes, passage_lengths, query_lengths, q, k, v)
    hidden_first = states.astype(f32) + project(mixed, whole_out) + w_out_bias
    first_unit, first_inverse = standardize(hidden_first)
    first_norm = first_unit * w_first_gain + w_first_shift
    first_low = first_norm.astype(bf16)
    inner_sum = project(first_low, whole_inner) + w_inner_bias
    activated, slope = gelu_and_slope(inner_sum)
    activated, slope = activated.astype(bf16), slope.astype(bf16)
    hidden_second = first_norm + project(activated, whole_down) + w_down_bias
    second_unit, second_inverse = standardize(hidden_second)
    final_norm = second_unit * w_second_gain + w_second_shift

    split = passages * passage_rows

    def valid_rows(count, length, lengths):
        return lax.broadcasted_iota(jnp.int32, (count, length), 1) < lengths[:, None]

    passage_valid = valid_rows(passages, passage_rows, passage_lengths)
    query_valid = valid_rows(queries, query_rows, query_lengths)
    passage_scale = 1.0 / passage_lengths.astype(f32)[:, None]
    query_scale = 1.0 / query_lengths.astype(f32)[:, None]
    own_passages = (
        jnp.sum(
            jnp.where(
                passage_valid[:, :, None],
                final_norm[:split].reshape(passages, passage_rows, width),
                0.0,
            ),
            axis=1,
        )
        * passage_scale
    )
    own_queries = (
        jnp.sum(
            jnp.where(
                query_valid[:, :, None],
                final_norm[split:].reshape(queries, query_rows, width),
                0.0,
            ),
            axis=1,
        )
        * query_scale
    )

    marks = jnp.pad(positive_index.astype(f32)[:, None], ((0, 0), (0, width - 1)))
    card = jnp.concatenate([own_queries, own_passages, marks], axis=0)
    deck = interleave(grid, gather_all(grid, card, "oi"), 0, card.shape[0])
    every_query = deck[:, :queries].reshape(total * queries, width)
    every_passage = deck[:, queries : queries + passages].reshape(total * passages, width)
    every_mark = deck[:, queries + passages :, 0].reshape(total * queries).astype(jnp.int32)
    query_units, _ = unit_rows(every_query)
    passage_units, _ = unit_rows(every_passage)
    logits = exact(query_units, passage_units, 1, 1) / sharpness_divisor
    chosen = lax.broadcasted_iota(jnp.int32, logits.shape, 1) == every_mark[:, None]
    log_total = jax.nn.logsumexp(logits, axis=1, keepdims=True)
    picked = jnp.sum(jnp.where(chosen, logits, 0.0), axis=1, keepdims=True)
    loss_value = jnp.mean(log_total - picked)
    logit_grad = (jnp.exp(logits - log_total) - chosen.astype(f32)) * (
        1.0 / (logits.shape[0] * sharpness_divisor)
    )
    me = (grid.o * grid.inner + grid.i) * 2 + grid.c
    own_rows = lax.dynamic_slice_in_dim(logit_grad, me * queries, queries, 0)
    own_columns = lax.dynamic_slice_in_dim(logit_grad, me * passages, passages, 1)
    query_embed_grad = unit_rows_back(
        exact(own_rows, passage_units, 1, 0), *unit_rows(own_queries)
    )
    passage_embed_grad = unit_rows_back(
        exact(own_columns, query_units, 0, 0), *unit_rows(own_passages)
    )

    spread = jnp.concatenate(
        [
            jnp.where(
                passage_valid[:, :, None], (passage_embed_grad * passage_scale)[:, None, :], 0.0
            ).reshape(split, width),
            jnp.where(
                query_valid[:, :, None], (query_embed_grad * query_scale)[:, None, :], 0.0
            ).reshape(queries * query_rows, width),
        ],
        axis=0,
    )
    second_gain_grad = jnp.sum(spread * second_unit, axis=0)
    second_shift_grad = jnp.sum(spread, axis=0)
    second_grad = standardize_back(spread * w_second_gain, second_unit, second_inverse)
    outer_low = second_grad.astype(bf16)
    down_weight_grad = weight_grad(activated, outer_low).astype(bf16)
    down_bias_grad = column_sum(outer_low)
    inner_low = (project_back(outer_low, whole_down) * slope.astype(f32)).astype(bf16)
    inner_weight_grad = weight_grad(first_low, inner_low).astype(bf16)
    inner_bias_grad = column_sum(inner_low)

    def spots(grad, count=1):
        return grad.reshape(grid.outer, grid.inner, 2, count * rows, width)

    inner_spots = inner_weight_grad.reshape(grid.outer, grid.inner, 2, rows, folds, width)
    down_spots = spots(down_weight_grad, folds)
    forward_one = jnp.concatenate(
        [inner_spots[..., j, :] for j in range(folds)] + [down_spots[..., :rows, :]], axis=3
    )
    forward_two = down_spots[..., rows:, :]
    forward_one_sum = scatter_sum(grid, forward_one, "io")
    forward_two_sum = scatter_sum(grid, forward_two, "oi")

    first_norm_grad = second_grad + project_back(inner_low, whole_inner)
    first_gain_grad = jnp.sum(first_norm_grad * first_unit, axis=0)
    first_shift_grad = jnp.sum(first_norm_grad, axis=0)
    first_grad = standardize_back(first_norm_grad * w_first_gain, first_unit, first_inverse)
    attended_low = first_grad.astype(bf16)
    out_weight_grad = weight_grad(mixed, attended_low).astype(bf16)
    out_bias_grad = column_sum(attended_low)
    mixed_low = project_back(attended_low, whole_out).astype(bf16)
    query_low, key_low, value_low = attention_backward(
        sizes, passage_lengths, query_lengths, q, k, v, mixed_low, lse
    )
    query_weight_grad = weight_grad(states, query_low).astype(bf16)
    key_weight_grad = weight_grad(states, key_low).astype(bf16)
    value_weight_grad = weight_grad(states, value_low).astype(bf16)
    input_grad = (
        first_grad
        + project_back(query_low, whole_query)
        + project_back(key_low, whole_key)
        + project_back(value_low, whole_value)
    ).astype(bf16)

    small_grads = [
        column_sum(query_low),
        column_sum(value_low),
        out_bias_grad,
        first_gain_grad,
        first_shift_grad,
        down_bias_grad,
        second_gain_grad,
        second_shift_grad,
        inner_bias_grad,
    ]
    small_grads = jnp.concatenate([g.reshape(total, -1) for g in small_grads], axis=1)
    small_grads = jnp.pad(
        small_grads.astype(bf16), ((0, 0), (0, pad_rows * width - small_grads.shape[1]))
    ).reshape(grid.outer, grid.inner, 2, pad_rows, width)
    attention_part = jnp.concatenate(
        [
            spots(query_weight_grad),
            spots(key_weight_grad),
            spots(value_weight_grad),
            small_grads,
        ],
        axis=3,
    )
    attention_sum = scatter_sum(grid, attention_part, "io")
    out_sum = scatter_sum(grid, spots(out_weight_grad), "oi")
    small_sum = attention_sum[3 * rows :].reshape(-1)

    def piece(j, count=1):
        return small_sum[j * rows : (j + count) * rows]

    inner_out = jnp.concatenate(
        [forward_one_sum[j * rows : (j + 1) * rows] for j in range(folds)], axis=1
    )
    down_out = jnp.concatenate([forward_one_sum[folds * rows :], forward_two_sum], axis=0)
    return (
        loss_value,
        own_queries,
        own_passages,
        input_grad[split:].reshape(query_states.shape),
        input_grad[:split].reshape(passage_states.shape),
        attention_sum[:rows],
        piece(0),
        attention_sum[rows : 2 * rows],
        attention_sum[2 * rows : 3 * rows],
        piece(1),
        out_sum,
        piece(2),
        piece(3),
        piece(4),
        inner_out,
        piece(8, folds),
        down_out,
        piece(5),
        piece(6),
        piece(7),
    )


def solution(mesh):
    flat, row, cube = P(AXIS), P(AXIS, None), P(AXIS, None, None)
    return jax.shard_map(
        functools.partial(on_device, mesh.shape[AXIS]),
        mesh=mesh,
        in_specs=(
            cube,
            cube,
            flat,
            flat,
            flat,
            row,
            flat,
            row,
            row,
            flat,
            row,
            flat,
            flat,
            flat,
            row,
            flat,
            row,
            flat,
            flat,
            flat,
        ),
        out_specs=(
            P(),
            row,
            row,
            cube,
            cube,
            row,
            flat,
            row,
            row,
            flat,
            row,
            flat,
            flat,
            flat,
            row,
            flat,
            row,
            flat,
            flat,
            flat,
        ),
        check_vma=False,
    )
```
